256 devices in a mesh: lon: 16 (over y, z_lo, core), lat: 16 (over x, z_hi).
Axes of the slice: x: 4, y: 4, z: 8 (z_hi: 4, z_lo: 2; z = z_hi * 2 + z_lo), core: 2. Of those that a mesh axis runs over, the one named last changes fastest.
Arguments:
- fine_state: bfloat16 [2048, 1024, 128], P('lon', 'lat'), may hold values from -6 to 6
- coarse_state: bfloat16 [128, 64, 512], P('lon', 'lat'), may hold values from -6 to 6
- norm_gains: float32 [2, 128], replicated, may hold values from 0.25 to 1.75
- kernels: bfloat16 [2, 3, 3, 128, 128], replicated, may hold values from -0.1875 to 0.1875
- token_gain: float32 [512], replicated, may hold values from 0.25 to 1.75
- head_gains: float32 [2, 64], replicated, may hold values from 1.2 to 2.2
- query_weight: bfloat16 [512, 512], replicated, may hold values from -0.25 to 0.25
- keyvalue_weight: bfloat16 [512, 1024], replicated, may hold values from -0.25 to 0.25
- output_weight: bfloat16 [512, 512], replicated, may hold values from -0.25 to 0.25
- expand_weight: bfloat16 [512, 128], replicated, may hold values from -0.25 to 0.25
Outputs:
- fine_result: bfloat16 [2048, 1024, 128], P('lon', 'lat')
- coarse_result: bfloat16 [128, 64, 512], P('lon', 'lat')
The draws below stay inside these ranges and needn't reach their ends.
All inputs are finite; a program needn't handle non-finite values.
Results may differ from the reference program's by a relative error of at most 0.005.
Values may be sent and summed in bfloat16 or wider, within the bound.
No kernel may reach another device: no remote copies, remote signals or barrier semaphores. Data moves between devices by JAX's collectives and lax.ppermute only.
A program may use at most 192 MiB of HBM per device.

```python
import math
import jax
import jax.numpy as jnp
from jax import lax

CH = 128
WIDTH = 512
HD = 64
HEADS = 8
PLON = 16
PLAT = 16
TDEV = 32
NLON = 2048
NLAT = 1024
GLON = 128
GLAT = 64
TOKENS = 8192


def level_of(stream_key, dims, pieces, low, largest):
    level = 1.0
    for axis_at, parts in pieces:
        steps = jax.random.uniform(jax.random.fold_in(jax.random.fold_in(stream_key, 6), axis_at), (parts,), jnp.float32, low / len(pieces), largest / len(pieces))
        level = level * jnp.repeat(jnp.exp(steps), dims[axis_at] // parts).reshape((-1,) + (1,) * (len(dims) - 1 - axis_at))
    return level


def scatter_about(key, dims, deviation, bound, cuts=(), dtype=jnp.bfloat16):
    values = jax.random.normal(key, dims, jnp.float32) * deviation
    if len(cuts) > 0:
        values = level_of(key, dims, cuts, -0.22, 0.18) * values
    return jnp.clip(values, min=-bound, max=bound).astype(dtype)


def setup_inputs(seed: int = 0) -> dict:
    seeds = jax.random.split(jax.random.key(seed), 11)
    fine_state = scatter_about(seeds[0], (NLON, NLAT, CH), 1.0, 6.0, ((0, 16), (1, 16)))
    coarse_state = scatter_about(seeds[1], (GLON, GLAT, WIDTH), 1.0, 6.0, ((0, 16), (1, 16)))
    norm_gains = jnp.clip(1.0 + 0.15 * jax.random.normal(seeds[2], (2, CH), jnp.float32), 0.25, 1.75)
    kernels = scatter_about(seeds[3], (2, 3, 3, CH, CH), (9 * CH) ** -0.5, 0.1875)
    token_gain = jnp.clip(1.0 + 0.15 * jax.random.normal(seeds[4], (WIDTH,), jnp.float32), 0.25, 1.75)
    head_gains = jnp.clip(jax.random.uniform(seeds[5], (2, HD), jnp.float32, 1.2, 2.2), 1.2, 2.2)
    query_weight = scatter_about(seeds[6], (WIDTH, WIDTH), WIDTH ** -0.5, 0.25)
    keyvalue_weight = scatter_about(seeds[7], (WIDTH, 2 * WIDTH), WIDTH ** -0.5, 0.25)
    output_weight = scatter_about(seeds[8], (WIDTH, WIDTH), WIDTH ** -0.5, 0.25)
    expand_weight = scatter_about(seeds[9], (WIDTH, CH), WIDTH ** -0.5, 0.25)
    return {"fine_state": fine_state, "coarse_state": coarse_state, "norm_gains": norm_gains, "kernels": kernels, "token_gain": token_gain, "head_gains": head_gains, "query_weight": query_weight, "keyvalue_weight": keyvalue_weight, "output_weight": output_weight, "expand_weight": expand_weight}


def rescale_rows(matrix, gain_row):
    return matrix * lax.rsqrt(lax.optimization_barrier(jnp.mean(matrix * matrix, axis=-1, keepdims=True)) + 1e-06) * gain_row

def rescale_heads(projected, gain_row):
    shaped = projected.reshape(projected.shape[0], HEADS, HD)
    return rescale_rows(shaped, gain_row)

def border_grid(hidden):
    wrapped = jnp.concatenate([hidden[-1:], hidden, hidden[:1]], axis=0)
    return jnp.pad(wrapped, ((0, 0), (1, 1), (0, 0)))

def convolve(padded, kernel):
    return lax.conv_general_dilated(padded[None], kernel, (1, 1), 'VALID', dimension_numbers=('NHWC', 'HWIO', 'NHWC'), preferred_element_type=jnp.float32)[0]

def reference(fine_state, coarse_state, norm_gains, kernels, token_gain, head_gains, query_weight, keyvalue_weight, output_weight, expand_weight):
    first_hidden = jax.nn.silu(rescale_rows(fine_state.astype(jnp.float32), norm_gains[0])).astype(jnp.bfloat16)
    first_output = convolve(border_grid(first_hidden), kernels[0])
    second_hidden = jax.nn.silu(rescale_rows(first_output, norm_gains[1])).astype(jnp.bfloat16)
    second_output = convolve(border_grid(second_hidden), kernels[1])
    tokens = coarse_state.reshape(TOKENS, WIDTH)
    normed = rescale_rows(tokens.astype(jnp.float32), token_gain).astype(jnp.bfloat16)
    scale_factor = 1.0 / math.sqrt(HD)
    queries = (rescale_heads(jnp.dot(normed, query_weight, preferred_element_type=jnp.float32), head_gains[0]) * scale_factor).astype(jnp.bfloat16)
    projected = jnp.dot(normed, keyvalue_weight, preferred_element_type=jnp.float32)
    key_rows = rescale_heads(projected[:, :WIDTH], head_gains[1]).astype(jnp.bfloat16)
    value_rows = projected[:, WIDTH:].astype(jnp.bfloat16).reshape(TOKENS, HEADS, HD)
    queries, key_rows, value_rows = lax.optimization_barrier((queries, key_rows, value_rows))
    key_wide = key_rows.astype(jnp.float32)
    value_wide = value_rows.astype(jnp.float32)

    def attend(query_block):
        scores = jnp.einsum('thd,shd->hts', query_block.astype(jnp.float32), key_wide)
        weights = jnp.exp(scores)
        totals = lax.optimization_barrier(jnp.sum(weights, axis=-1))
        rounded = lax.optimization_barrier(weights.astype(jnp.bfloat16)).astype(jnp.float32)
        summed = jnp.einsum('hts,shd->thd', rounded, value_wide)
        return (summed / jnp.transpose(totals)[:, :, None]).astype(jnp.bfloat16)
    query_blocks = queries.reshape(TOKENS // TDEV, TDEV, HEADS, HD)
    attended = lax.map(attend, query_blocks).reshape(TOKENS, WIDTH)
    coarse_result = (tokens.astype(jnp.float32) + jnp.dot(attended, output_weight, preferred_element_type=jnp.float32)).astype(jnp.bfloat16)
    lifted = jnp.dot(coarse_result, expand_weight, preferred_element_type=jnp.float32).reshape(GLON, 1, GLAT, 1, CH)
    merged = (fine_state.astype(jnp.float32) + second_output).reshape(GLON, PLON, GLAT, PLAT, CH) + lifted
    fine_result = merged.reshape(NLON, NLAT, CH).astype(jnp.bfloat16)
    return (fine_result, coarse_result.reshape(GLON, GLAT, WIDTH))
```

```python
import math

import jax
import jax.numpy as jnp
from jax import lax
from jax.sharding import PartitionSpec as P

AXES = ("lon", "lat")


def device_pairs(move):
    pairs = []
    for y in range(4):
        for zl in range(2):
            for c in range(2):
                for x in range(4):
                    for zh in range(4):
                        ty, tl, tc, tx, th = move(y, zl, c, x, zh)
                        source = ((y * 2 + zl) * 2 + c) * 16 + x * 4 + zh
                        target = (((ty % 4) * 2 + tl % 2) * 2 + tc % 2) * 16 + (tx % 4) * 4 + th % 4
                        pairs.append((source, target))
    return pairs


def move_core(value):
    return lax.ppermute(value, AXES, device_pairs(lambda y, l, c, x, h: (y, l, c + 1, x, h)))


def move_low(value):
    return lax.ppermute(value, AXES, device_pairs(lambda y, l, c, x, h: (y, l + 1, c, x, h)))


def move_y(value, k):
    return lax.ppermute(value, AXES, device_pairs(lambda y, l, c, x, h: (y + k, l, c, x, h)))


def move_x(value, k):
    return lax.ppermute(value, AXES, device_pairs(lambda y, l, c, x, h: (y, l, c, x + k, h)))


def move_high(value, k):
    return lax.ppermute(value, AXES, device_pairs(lambda y, l, c, x, h: (y, l, c, x, h + k)))


def rescale_rows(matrix, gain_row):
    return matrix * lax.rsqrt(jnp.mean(matrix * matrix, axis=-1, keepdims=True) + 1e-06) * gain_row


def rescale_heads(projected, gain_row):
    shaped = projected.reshape(projected.shape[0], -1, gain_row.shape[0])
    return rescale_rows(shaped, gain_row)


def convolve(padded, kernel):
    return lax.conv_general_dilated(
        padded[None],
        kernel,
        (1, 1),
        "VALID",
        dimension_numbers=("NHWC", "HWIO", "NHWC"),
        preferred_element_type=jnp.float32,
    )[0]


def attach_rims(block, width):
    count = 16
    forward = [(i, (i + 1) % count) for i in range(count)]
    backward = [(b, a) for a, b in forward]
    low = lax.ppermute(block[-width:], "lon", forward)
    high = lax.ppermute(block[:width], "lon", backward)
    block = jnp.concatenate([low, block, high], axis=0)
    low = lax.ppermute(block[:, -width:], "lat", forward[:-1])
    high = lax.ppermute(block[:, :width], "lat", backward[:-1])
    return jnp.concatenate([low, block, high], axis=1)


def gather_queries(tokens):
    block = jnp.concatenate([tokens] + [move_y(tokens, -k) for k in (1, 2, 3)], axis=0)
    block = jnp.concatenate([block, move_low(block)], axis=0)
    return jnp.concatenate([block, move_core(block)], axis=0)


def gather_keys(tokens):
    block = jnp.concatenate([tokens] + [move_high(tokens, k) for k in (1, 2, 3)], axis=0)
    return jnp.concatenate([block] + [move_x(block, k) for k in (1, 2, 3)], axis=0)


def pack(partial):
    summed, totals = partial
    high = totals.astype(jnp.bfloat16)
    low = (totals - high.astype(jnp.float32)).astype(jnp.bfloat16)
    pad = jnp.zeros((summed.shape[0], 112), jnp.bfloat16)
    return jnp.concatenate([summed.astype(jnp.bfloat16), high, low, pad], axis=1)


def add_packed(partial, packed):
    summed, totals = partial
    packed = packed.astype(jnp.float32)
    return summed + packed[:, :512], totals + packed[:, 512:520] + packed[:, 520:528]


def split(partial, low, high):
    return partial[0][low:high], partial[1][low:high]


def reduce_partials(partial):
    received = move_core(pack(split(partial, 256, 512)))
    partial = add_packed(split(partial, 0, 256), received)
    received = move_low(pack(split(partial, 128, 256)))
    partial = add_packed(split(partial, 0, 128), received)
    received = [move_y(pack(split(partial, 32 * k, 32 * k + 32)), k) for k in (1, 2, 3)]
    partial = split(partial, 0, 32)
    for packed in received:
        partial = add_packed(partial, packed)
    return partial


def local(
    fine_state,
    coarse_state,
    norm_gains,
    kernels,
    token_gain,
    head_gains,
    query_weight,
    keyvalue_weight,
    output_weight,
    expand_weight,
):
    width_all = query_weight.shape[0]
    head_size = head_gains.shape[1]
    head_count = width_all // head_size
    lon_tokens = coarse_state.shape[0]
    lat_tokens = coarse_state.shape[1]
    lon_cells, lat_cells, channels = fine_state.shape
    tokens = coarse_state.reshape(-1, width_all)
    query_tokens = gather_queries(tokens)
    key_tokens = gather_keys(tokens)
    wide = attach_rims(fine_state, 2)

    first_hidden = jax.nn.silu(rescale_rows(wide.astype(jnp.float32), norm_gains[0])).astype(
        jnp.bfloat16
    )
    first_output = convolve(first_hidden, kernels[0])
    second_hidden = jax.nn.silu(rescale_rows(first_output, norm_gains[1]))
    column = lax.axis_index("lat") * lat_cells - 1 + lax.broadcasted_iota(
        jnp.int32, (1, lat_cells + 2, 1), 1
    )
    inside = (column >= 0) & (column < lat_cells * lax.axis_size("lat"))
    second_hidden = jnp.where(inside, second_hidden, 0.0).astype(jnp.bfloat16)
    second_output = convolve(second_hidden, kernels[1])

    scale_factor = 1.0 / math.sqrt(head_size)
    normed = rescale_rows(query_tokens.astype(jnp.float32), token_gain).astype(jnp.bfloat16)
    queries = (
        rescale_heads(
            jnp.dot(normed, query_weight, preferred_element_type=jnp.float32), head_gains[0]
        )
        * scale_factor
    ).astype(jnp.bfloat16)
    normed = rescale_rows(key_tokens.astype(jnp.float32), token_gain).astype(jnp.bfloat16)
    projected = jnp.dot(normed, keyvalue_weight, preferred_element_type=jnp.float32)
    key_heads = rescale_heads(projected[:, :width_all], head_gains[1]).astype(jnp.bfloat16)
    value_heads = projected[:, width_all:].astype(jnp.bfloat16).reshape(-1, head_count, head_size)
    scores = jnp.einsum("thd,shd->hts", queries, key_heads, preferred_element_type=jnp.float32)
    weights = jnp.exp(scores)
    totals = jnp.transpose(jnp.sum(weights, axis=-1))
    summed = jnp.einsum(
        "hts,shd->thd",
        weights.astype(jnp.bfloat16),
        value_heads,
        preferred_element_type=jnp.float32,
    ).reshape(-1, width_all)
    summed, totals = reduce_partials((summed, totals))
    attended = (
        (summed.reshape(-1, head_count, head_size) / totals[:, :, None])
        .reshape(-1, width_all)
        .astype(jnp.bfloat16)
    )
    coarse_result = (
        tokens.astype(jnp.float32)
        + jnp.dot(attended, output_weight, preferred_element_type=jnp.float32)
    ).astype(jnp.bfloat16)
    lifted = jnp.dot(coarse_result, expand_weight, preferred_element_type=jnp.float32).reshape(
        lon_tokens, 1, lat_tokens, 1, channels
    )
    merged = (fine_state.astype(jnp.float32) + second_output).reshape(
        lon_tokens, lon_cells // lon_tokens, lat_tokens, lat_cells // lat_tokens, channels
    ) + lifted
    fine_result = merged.reshape(lon_cells, lat_cells, channels).astype(jnp.bfloat16)
    return (fine_result, coarse_result.reshape(lon_tokens, lat_tokens, width_all))


def solution(mesh):
    return jax.shard_map(
        local,
        mesh=mesh,
        in_specs=(
            P("lon", "lat", None),
            P("lon", "lat", None),
            P(),
            P(),
            P(),
            P(),
            P(),
            P(),
            P(),
            P(),
        ),
        out_specs=(P("lon", "lat", None), P("lon", "lat", None)),
        check_vma=False,
    )
```

```python
import functools
import math
import jax
import jax.numpy as jnp
from jax import lax
from jax.experimental import pallas as pl
from jax.experimental.pallas import tpu as pltpu

from jax.sharding import PartitionSpec as P


WIDE = 80
CIRCLE = 72
NORM_UNROLL = 2
CONV_UNROLL = 1
SHIFT_UNROLL = 4
CONV2_UNROLL = 1
F32 = jnp.float32
BF16 = jnp.bfloat16


def unit_rows(v, gain):
    return v * lax.rsqrt(jnp.mean(v * v, axis=-1, keepdims=True) + 1e-06) * gain


def silu(v):
    half = v * 0.5
    return half + half * jnp.tanh(half)


def pair_weights(taps_ref, which, pair_ref):
    zero = jnp.zeros((128, 128), BF16)
    for row in range(4):
        for b in range(3):
            at = (row * 3 + b) * 128
            pair_ref[at : at + 128, 0:128] = taps_ref[which, row, b] if row < 3 else zero
            pair_ref[at : at + 128, 128:256] = taps_ref[which, row - 1, b] if row > 0 else zero


def store_shifted(hidden_ref, p, value, width):
    hidden_ref[0, p, :, :width] = pltpu.roll(value, 1, 1)[:, :width].astype(BF16)
    hidden_ref[1, p, :, :width] = value[:, :width].astype(BF16)
    hidden_ref[2, p, :, :width] = pltpu.roll(value, CIRCLE - 1, 1)[:, :width].astype(BF16)


def conv_pairs(hidden_ref, pair_ref, first, count, width):
    pieces = []
    for row in range(4):
        for b in range(3):
            piece = hidden_ref[b, pl.ds(first + row // 2, count), row % 2]
            pieces.append(piece.reshape(count * width, 128))
    return jnp.dot(
        jnp.concatenate(pieces, axis=1), pair_ref[...], preferred_element_type=F32
    )


def first_conv_kernel(begin, count, fine_ref, low_ref, high_ref, rim_ref, taps_ref, gains_ref, inside_ref, out_ref, hidden_ref, pair_ref):
    pair_weights(taps_ref, 0, pair_ref)
    gain = gains_ref[0:1, :].reshape(1, 1, 128)

    def activate(main, rim, p):
        row = jnp.concatenate([main.astype(F32), rim.astype(F32)], axis=1)
        store_shifted(hidden_ref, p - begin, silu(unit_rows(row, gain)), CIRCLE)

    lower, upper = begin, begin + count + 1
    if lower == 0:
        activate(low_ref[...], rim_ref[0:2], 0)
        lower = 1
    if upper == 66:
        activate(high_ref[...], rim_ref[130:132], 65)
        upper = 65

    def norm_step(p, carry):
        activate(fine_ref[pl.ds(2 * p - 2, 2)], rim_ref[pl.ds(2 * p, 2)], p)
        return carry

    lax.fori_loop(lower, upper, norm_step, 0, unroll=NORM_UNROLL)
    second_gain = gains_ref[1:2, :].reshape(1, 1, 128)
    inside = inside_ref[...].reshape(1, CIRCLE, 128)

    def conv_step(i, carry):
        first = i * 5
        both = conv_pairs(hidden_ref, pair_ref, first, 5, WIDE)
        for half in range(2):
            value = both[:, 128 * half : 128 * half + 128].reshape(5, WIDE, 128)[:, :CIRCLE]
            value = silu(unit_rows(value, second_gain)) * inside
            out_ref[pl.ds(first, 5), half] = value.astype(BF16)
        return carry

    lax.fori_loop(0, count // 5, conv_step, 0, unroll=CONV_UNROLL)


VMEM_SPEC = pl.BlockSpec(memory_space=pltpu.VMEM)


def first_conv(begin, count, fine, low, high, rim, kernels, gains, inside):
    return pl.pallas_call(
        functools.partial(first_conv_kernel, begin, count),
        out_shape=jax.ShapeDtypeStruct((count, 2, CIRCLE, 128), BF16),
        in_specs=[VMEM_SPEC] * 7,
        out_specs=VMEM_SPEC,
        scratch_shapes=[pltpu.VMEM((3, count + 1, 2, WIDE, 128), BF16), pltpu.VMEM((1536, 256), BF16)],
        compiler_params=pltpu.CompilerParams(vmem_limit_bytes=14 << 20),
        name="first_conv",
    )(fine, low, high, rim, kernels, gains, inside)


def second_conv_kernel(begin, pairs, split_at, *refs):
    hidden_refs, (taps_ref, fine_ref, out_ref, hidden_ref, pair_ref) = refs[:-5], refs[-5:]
    pair_weights(taps_ref, 1, pair_ref)
    lower = begin
    for ref, stop, offset in zip(hidden_refs, (split_at, begin + pairs + 1), (0, split_at)):
        upper = min(stop, begin + pairs + 1)

        def shift_step(p, carry, ref=ref, offset=offset):
            store_shifted(hidden_ref, p - begin, ref[p - offset].astype(F32), 64)
            return carry

        if upper > lower:
            lax.fori_loop(lower, upper, shift_step, 0, unroll=SHIFT_UNROLL)
            lower = upper

    def conv_step(i, carry):
        first = i * 8
        both = conv_pairs(hidden_ref, pair_ref, first, 8, 64)
        for half in range(2):
            value = both[:, 128 * half : 128 * half + 128].reshape(8, 64, 128)
            out_ref[pl.ds(first, 8), half] = value + fine_ref[pl.ds(begin + first, 8), half].astype(F32)
        return carry

    lax.fori_loop(0, pairs // 8, conv_step, 0, unroll=CONV2_UNROLL)


def second_conv(begin, pairs, hidden, kernels, fine):
    split_at = hidden[0].shape[0]
    return pl.pallas_call(
        functools.partial(second_conv_kernel, begin, pairs, split_at),
        out_shape=jax.ShapeDtypeStruct((pairs, 2, 64, 128), F32),
        in_specs=[VMEM_SPEC] * (len(hidden) + 2),
        out_specs=VMEM_SPEC,
        scratch_shapes=[pltpu.VMEM((3, pairs + 1, 2, 64, 128), BF16), pltpu.VMEM((1536, 256), BF16)],
        compiler_params=pltpu.CompilerParams(vmem_limit_bytes=12 << 20),
        name="second_conv",
    )(*hidden, kernels, fine.reshape(64, 2, 64, 128))


def high_low(v):
    high = v.astype(BF16)
    return high, (v - high.astype(F32)).astype(BF16)


def attention_kernel(q0_ref, q1_ref, k0_ref, k1_ref, k2_ref, k3_ref, gain_ref, head_ref, wq_ref, wkv_ref, keep_ref, send_ref):
    gain = gain_ref[...]
    lane = lax.broadcasted_iota(jnp.int32, (1, 128), 1)
    r = lax.broadcasted_iota(jnp.int32, (256, 128), 0)
    c = lax.broadcasted_iota(jnp.int32, (256, 128), 1)
    block = jnp.where(((r % 128) // 64) == (c // 64), 1.0 / 64, 0.0).astype(BF16)
    even = lane < 64

    def head_norm(v, head_gain):
        high, low = high_low(v * v)
        mean = jnp.dot(jnp.concatenate([high, low], axis=1), block, preferred_element_type=F32)
        return v * lax.rsqrt(mean + 1e-06) * head_gain

    query_rows = jnp.concatenate([q0_ref[...], q1_ref[...]], axis=0).astype(F32)
    query_rows = unit_rows(query_rows, gain).astype(BF16)
    key_rows = jnp.concatenate([k0_ref[...], k1_ref[...], k2_ref[...], k3_ref[...]], axis=0).astype(F32)
    key_rows = unit_rows(key_rows, gain).astype(BF16)
    scale = 1.0 / math.sqrt(64)
    totals = jnp.zeros((512, 128), F32)
    for g in range(4):
        at = 128 * g
        q = jnp.dot(query_rows, wq_ref[:, at : at + 128], preferred_element_type=F32)
        q = (head_norm(q, head_ref[0:1, :]) * scale).astype(BF16)
        k = jnp.dot(key_rows, wkv_ref[:, at : at + 128], preferred_element_type=F32)
        k = head_norm(k, head_ref[1:2, :])
        v = jnp.dot(key_rows, wkv_ref[:, 512 + at : 640 + at], preferred_element_type=F32)
        parts = []
        for side in range(2):
            own = even if side == 0 else jnp.logical_not(even)
            k_own = jnp.where(own, k, 0.0).astype(BF16)
            v_own = jnp.where(own, v, 1.0).astype(BF16)
            scores = lax.dot_general(q, k_own, (((1,), (1,)), ((), ())), preferred_element_type=F32)
            weights = jnp.exp(scores).astype(BF16)
            parts.append(jnp.dot(weights, v_own, preferred_element_type=F32))
        summed = jnp.where(even, parts[0], parts[1])
        total = jnp.where(even, parts[1], parts[0])
        high = total.astype(BF16).astype(F32)
        totals = totals + jnp.where(lane % 64 == 2 * g, high, jnp.where(lane % 64 == 2 * g + 1, total - high, 0.0))
        keep_ref[:, at : at + 128] = summed[0:256]
        send_ref[:, at : at + 128] = summed[256:512].astype(BF16)
    keep_ref[:, 512:640] = totals[0:256]
    send_ref[:, 512:640] = totals[256:512].astype(BF16)


def attention(q0, q1, ks, token_gain, head_gains, wq, wkv):
    full = lambda shape: pl.BlockSpec(shape, lambda: (0,) * len(shape))
    head2 = jnp.concatenate([head_gains, head_gains], axis=1)
    return pl.pallas_call(
        attention_kernel,
        out_shape=(jax.ShapeDtypeStruct((256, 640), F32), jax.ShapeDtypeStruct((256, 640), BF16)),
        in_specs=[full((256, 512))] * 2 + [full((128, 512))] * 4 + [full((1, 512)), full((2, 128)), full((512, 512)), full((512, 1024))],
        out_specs=(full((256, 640)), full((256, 640))),
        compiler_params=pltpu.CompilerParams(vmem_limit_bytes=16 << 20),
        name="attention",
    )(q0, q1, *ks, token_gain.reshape(1, 512), head2, wq, wkv)


def split_totals(x):
    lane = lax.broadcasted_iota(jnp.int32, (1, 128), 1)
    total = x + pltpu.roll(x, 127, 1)
    high = total.astype(BF16).astype(F32)
    return jnp.where(lane % 2 == 0, high, pltpu.roll(total - high, 1, 1))


def reduce_kernel(keep_ref, got_ref, out_ref, send_ref):
    rows = out_ref.shape[0]
    total = keep_ref[...] + got_ref[...].astype(F32)
    out_ref[...] = total[:rows]
    send_ref[:, :512] = total[rows:, :512].astype(BF16)
    send_ref[:, 512:] = split_totals(total[rows:, 512:]).astype(BF16)


def reduce_step(keep, got, rows):
    count = keep.shape[0]
    full = lambda shape: pl.BlockSpec(shape, lambda: (0,) * len(shape))
    return pl.pallas_call(
        reduce_kernel,
        out_shape=(jax.ShapeDtypeStruct((rows, 640), F32), jax.ShapeDtypeStruct((count - rows, 640), BF16)),
        in_specs=[full((count, 640))] * 2,
        out_specs=(full((rows, 640)), full((count - rows, 640))),
        compiler_params=pltpu.CompilerParams(vmem_limit_bytes=4 << 20),
        name="reduce_step",
    )(keep, got)


def final_kernel(keep_ref, g1_ref, g2_ref, g3_ref, tokens_ref, wo_ref, we_ref, s0_ref, s1_ref, out_ref, coarse_ref, lifted_ref, block_ref, sems):
    total = keep_ref[...] + g1_ref[...].astype(F32) + g2_ref[...].astype(F32) + g3_ref[...].astype(F32)
    r = lax.broadcasted_iota(jnp.int32, (128, 512), 0)
    head = lax.broadcasted_iota(jnp.int32, (128, 512), 1) // 64
    at = jnp.where(head % 2 == 1, 0, 64) + head // 2 * 2
    pick = jnp.where((r == at) | (r == at + 1), 1.0, 0.0).astype(BF16)
    high, low = high_low(total[:, 512:])
    spread = jnp.dot(high, pick, preferred_element_type=F32) + jnp.dot(low, pick, preferred_element_type=F32)
    attended = (total[:, :512] / spread).astype(BF16)
    coarse = tokens_ref[...].astype(F32) + jnp.dot(attended, wo_ref[...], preferred_element_type=F32)
    rounded = coarse.astype(BF16)
    lifted_ref[...] = jnp.dot(rounded, we_ref[...], preferred_element_type=F32)
    for a in range(8):
        coarse_ref[a] = coarse[4 * a : 4 * a + 4].astype(BF16)
    copies = []
    for a in range(8):
        for b in range(4):
            row = lifted_ref[4 * a + b : 4 * a + b + 1, :].reshape(1, 1, 128)
            cols = slice(16 * b, 16 * b + 16)
            half_ref, at = (s0_ref, 16 * a) if a < 4 else (s1_ref, 16 * a - 64)
            block_ref[a, :, cols] = (half_ref[at : at + 16, cols] + row).astype(BF16)
        copy = pltpu.make_async_copy(block_ref.at[a], out_ref.at[pl.ds(16 * a, 16)], sems.at[a])
        copy.start()
        copies.append(copy)
    for copy in copies:
        copy.wait()


def final(keep, got, tokens, wo, we, second):
    return pl.pallas_call(
        final_kernel,
        out_shape=(jax.ShapeDtypeStruct((128, 64, 128), BF16), jax.ShapeDtypeStruct((8, 4, 512), BF16)),
        in_specs=[VMEM_SPEC] * 9,
        out_specs=(pl.BlockSpec(memory_space=pl.ANY), VMEM_SPEC),
        scratch_shapes=[pltpu.VMEM((32, 128), F32), pltpu.VMEM((8, 16, 64, 128), BF16), pltpu.SemaphoreType.DMA((8,))],
        compiler_params=pltpu.CompilerParams(vmem_limit_bytes=12 << 20),
        name="final",
    )(keep, *got, tokens, wo, we, *second)


AXES = ("lon", "lat")


def device_pairs(move):
    pairs = []
    for y in range(4):
        for zl in range(2):
            for c in range(2):
                for x in range(4):
                    for zh in range(4):
                        ty, tl, tc, tx, th = move(y, zl, c, x, zh)
                        source = ((y * 2 + zl) * 2 + c) * 16 + x * 4 + zh
                        target = (((ty % 4) * 2 + tl % 2) * 2 + tc % 2) * 16 + (tx % 4) * 4 + th % 4
                        pairs.append((source, target))
    return pairs


def move(value, y=0, low=0, core=0, x=0, high=0):
    return lax.ppermute(
        value, AXES,
        device_pairs(lambda a, b, c, d, e: (a + y, b + low, c + core, d + x, e + high)),
    )


def block(
    fine_state,
    coarse_state,
    norm_gains,
    kernels,
    token_gain,
    head_gains,
    query_weight,
    keyvalue_weight,
    output_weight,
    expand_weight,
):
    count = 16
    forward = [(i, (i + 1) % count) for i in range(count)]
    backward = [(b, a) for a, b in forward]
    low = lax.ppermute(fine_state[-2:], "lon", forward)
    high = lax.ppermute(fine_state[:2], "lon", backward)
    tokens = coarse_state.reshape(32, 512)
    far = [tokens] + [move(tokens, high=k) for k in (1, 2, 3)]
    first = jnp.concatenate([low[:, :2], fine_state[:, :2], high[:, :2]], axis=0)
    last = jnp.concatenate([low[:, -2:], fine_state[:, -2:], high[:, -2:]], axis=0)
    left = lax.ppermute(last, "lat", forward[:-1])
    right = lax.ppermute(first, "lat", backward[:-1])
    near = [tokens] + [move(tokens, y=-k) for k in (1, 2, 3)]
    rim = jnp.concatenate([right, jnp.zeros((132, 4, 128), BF16), left], axis=1)
    position = lax.broadcasted_iota(jnp.int32, (CIRCLE, 128), 0)
    column = lax.axis_index("lat") * 64 + jnp.where(position < 68, position, position - CIRCLE)
    inside = jnp.where((column >= 0) & (column < 64 * count), 1.0, 0.0).astype(F32)
    hidden_a = first_conv(0, 35, fine_state, low, high, rim, kernels, norm_gains, inside)

    far = jnp.concatenate(far, axis=0)
    key_tokens = [far] + [move(far, x=k) for k in (1, 2, 3)]
    near = jnp.concatenate(near, axis=0)
    near = jnp.concatenate([near, move(near, low=1)], axis=0)
    hidden_b = first_conv(35, 30, fine_state, low, high, rim, kernels, norm_gains, inside)
    across = move(near, core=1)
    keep, out = attention(near, across, key_tokens, token_gain, head_gains, query_weight, keyvalue_weight)
    keep, out = reduce_step(keep, move(out, core=1), 128)
    got = move(out, low=1)
    second_a = second_conv(0, 32, (hidden_a,), kernels, fine_state)
    keep, out = reduce_step(keep, got, 32)
    got = [move(out[32 * k - 32 : 32 * k], y=k) for k in (1, 2, 3)]
    second_b = second_conv(32, 32, (hidden_a, hidden_b), kernels, fine_state)
    second = [half.reshape(64, 64, 128) for half in (second_a, second_b)]
    return final(keep, got, tokens, output_weight, expand_weight, second)


def solution(mesh):
    return jax.shard_map(
        block,
        mesh=mesh,
        in_specs=(
            P("lon", "lat", None),
            P("lon", "lat", None),
            P(),
            P(),
            P(),
            P(),
            P(),
            P(),
            P(),
            P(),
        ),
        out_specs=(P("lon", "lat", None), P("lon", "lat", None)),
        check_vma=False,
    )
```

```python
import functools
import math
import jax
import jax.numpy as jnp
from jax import lax
from jax.experimental import pallas as pl
from jax.experimental.pallas import tpu as pltpu

from jax.sharding import PartitionSpec as P


WIDE = 80
CIRCLE = 72
SHIFT_BLOCK = 5
F32 = jnp.float32
BF16 = jnp.bfloat16


def unit_rows(v, gain):
    return v * lax.rsqrt(jnp.mean(v * v, axis=-1, keepdims=True) + 1e-06) * gain


def pair_weights(taps_ref, pair_ref):
    zero = jnp.zeros((128, 128), BF16)
    for row in range(4):
        for b in range(3):
            at = (row * 3 + b) * 128
            pair_ref[at : at + 128, 0:128] = taps_ref[row, b] if row < 3 else zero
            pair_ref[at : at + 128, 128:256] = taps_ref[row - 1, b] if row > 0 else zero


def activate_rows(v, half_gain):
    half = v * (lax.rsqrt(jnp.mean(v * v, axis=-1, keepdims=True) + 1e-06) * half_gain)
    return half + half * jnp.tanh(half)


def store_shifted(hidden_ref, p, count, half, value, width):
    at = pl.ds(p, count)
    hidden_ref[0, at, half, :width] = pltpu.roll(value, 1, 1)[:, :width].astype(BF16)
    hidden_ref[1, at, half, :width] = value[:, :width].astype(BF16)
    hidden_ref[2, at, half, :width] = pltpu.roll(value, CIRCLE - 1, 1)[:, :width].astype(BF16)


def conv_pairs(hidden_ref, pair_ref, first, count, width):
    pieces = []
    for row in range(4):
        for b in range(3):
            at = first + row // 2
            piece = hidden_ref[b, at : at + count, row % 2]
            pieces.append(piece.reshape(count * width, 128))
    return jnp.dot(
        jnp.concatenate(pieces, axis=1), pair_ref[...], preferred_element_type=F32
    )


def first_conv_kernel(begin, count, fine_ref, low_ref, high_ref, rim_ref, taps_ref, gains_ref, inside_ref, out_ref, hidden_ref, pair_ref, *own):
    lower, upper = max(begin, 1), min(begin + count + 1, 65)
    block = next(n for n in (5, 7) if (upper - lower) % n == 0)
    bounds = list(range(lower, upper + 1, block))
    copies, rows_ref, first_row = [], fine_ref, 2
    taps, gains = taps_ref.at[0], gains_ref
    if own:
        rows_ref, taps, gains, sems = own
        first_row = 2 * lower
        gain_copy = pltpu.make_async_copy(gains_ref, gains, sems.at[0])
        gain_copy.start()
        for k in range(len(bounds) - 1):
            size = 2 * (bounds[k + 1] - bounds[k])
            copy = pltpu.make_async_copy(
                fine_ref.at[pl.ds(2 * bounds[k] - 2, size)],
                rows_ref.at[pl.ds(2 * (bounds[k] - lower), size)],
                sems.at[2 + k],
            )
            copy.start()
            copies.append(copy)
        taps_copy = pltpu.make_async_copy(taps_ref.at[0], taps, sems.at[1])
        taps_copy.start()
        gain_copy.wait()
    half_gain = 0.5 * gains[0:1, :].reshape(1, 1, 128)

    def activate(main, rim, p, count):
        row = jnp.concatenate([main.astype(F32), rim.astype(F32)], axis=1)
        row = activate_rows(row, half_gain).reshape(count, 2, CIRCLE, 128)
        for half in range(2):
            store_shifted(hidden_ref, p - begin, count, half, row[:, half], CIRCLE)

    if begin == 0:
        activate(low_ref[...], rim_ref[0:2], 0, 1)
    if begin + count == 65:
        activate(high_ref[...], rim_ref[130:132], 65, 1)
    for k, p in enumerate(bounds[:-1]):
        if own:
            copies[k].wait()
        at = 2 * p - first_row
        activate(rows_ref[at : at + 2 * block], rim_ref[2 * p : 2 * p + 2 * block], p, block)
    if own:
        taps_copy.wait()
    pair_weights(taps, pair_ref)
    second_half_gain = 0.5 * gains[1:2, :].reshape(1, 1, 128)
    inside = inside_ref[...].reshape(1, CIRCLE, 128)
    for first in range(0, count, 5):
        both = conv_pairs(hidden_ref, pair_ref, first, 5, WIDE)
        for half in range(2):
            value = both[:, 128 * half : 128 * half + 128].reshape(5, WIDE, 128)[:, :CIRCLE]
            value = activate_rows(value, second_half_gain) * inside
            out_ref[first : first + 5, half] = value.astype(BF16)


VMEM_SPEC = pl.BlockSpec(memory_space=pltpu.VMEM)
ANY_SPEC = pl.BlockSpec(memory_space=pl.ANY)


def first_conv(begin, count, fine, low, high, rim, kernels, gains, inside):
    lower, upper = max(begin, 1), min(begin + count + 1, 65)
    place, scratch = VMEM_SPEC, []
    if begin == 0:
        place = ANY_SPEC
        scratch = [
            pltpu.VMEM((2 * (upper - lower), 64, 128), BF16),
            pltpu.VMEM((3, 3, 128, 128), BF16),
            pltpu.VMEM((2, 128), F32),
            pltpu.SemaphoreType.DMA((2 + 5,)),
        ]
    return pl.pallas_call(
        functools.partial(first_conv_kernel, begin, count),
        out_shape=jax.ShapeDtypeStruct((count, 2, CIRCLE, 128), BF16),
        in_specs=[place, VMEM_SPEC, VMEM_SPEC, VMEM_SPEC, place, place, VMEM_SPEC],
        out_specs=VMEM_SPEC,
        scratch_shapes=[
            pltpu.VMEM((3, count + 1, 2, WIDE, 128), BF16),
            pltpu.VMEM((1536, 256), BF16),
        ] + scratch,
        compiler_params=pltpu.CompilerParams(vmem_limit_bytes=12 << 20),
        name="first_conv",
    )(fine, low, high, rim, kernels, gains, inside)


def second_conv_kernel(begin, pairs, starts, *refs):
    hidden_refs, (taps_ref, fine_ref, out_ref, hidden_ref, pair_ref) = refs[:-5], refs[-5:]
    pair_weights(taps_ref.at[1], pair_ref)
    for ref, start in zip(hidden_refs, starts):
        lower, upper = max(start, begin), min(start + ref.shape[0], begin + pairs + 1)
        for p in range(lower, upper, SHIFT_BLOCK):
            count = min(SHIFT_BLOCK, upper - p)
            for half in range(2):
                value = ref[p - start : p - start + count, half].astype(F32)
                store_shifted(hidden_ref, p - begin, count, half, value, 64)

    for first in range(0, pairs, 8):
        both = conv_pairs(hidden_ref, pair_ref, first, 8, 64)
        for half in range(2):
            value = both[:, 128 * half : 128 * half + 128].reshape(8, 64, 128)
            out_ref[first : first + 8, half] = value + fine_ref[begin + first : begin + first + 8, half].astype(F32)


def second_conv(begin, pairs, starts, hidden, kernels, fine):
    return pl.pallas_call(
        functools.partial(second_conv_kernel, begin, pairs, starts),
        out_shape=jax.ShapeDtypeStruct((pairs, 2, 64, 128), F32),
        in_specs=[VMEM_SPEC] * (len(hidden) + 2),
        out_specs=VMEM_SPEC,
        scratch_shapes=[pltpu.VMEM((3, pairs + 1, 2, 64, 128), BF16), pltpu.VMEM((1536, 256), BF16)],
        compiler_params=pltpu.CompilerParams(vmem_limit_bytes=12 << 20),
        name="second_conv",
    )(*hidden, kernels, fine.reshape(64, 2, 64, 128))


def high_low(v):
    high = v.astype(BF16)
    return high, (v - high.astype(F32)).astype(BF16)


def split_blocks(value, keep_ref, send_ref, columns):
    for i in range(value.shape[0] // 64):
        keep_ref[32 * i : 32 * i + 32, columns] = value[64 * i : 64 * i + 32]
        send_ref[32 * i : 32 * i + 32, columns] = value[64 * i + 32 : 64 * i + 64].astype(BF16)


def attention_kernel(q0_ref, q1_ref, k0_ref, k1_ref, gain_ref, head_ref, wq_ref, wkv_ref, keep_ref, send_ref):
    gain = gain_ref[...]
    lane = lax.broadcasted_iota(jnp.int32, (1, 128), 1)
    even = lane < 64

    def head_norm(v, head_gain):
        square = v * v
        sums = [jnp.sum(jnp.where(own, square, 0.0), axis=-1, keepdims=True) for own in (even, jnp.logical_not(even))]
        mean = jnp.where(even, sums[0], sums[1]) * (1.0 / 64)
        return v * lax.rsqrt(mean + 1e-06) * head_gain

    query_rows = jnp.concatenate([q0_ref[...], q1_ref[...]], axis=0).astype(F32)
    query_rows = unit_rows(query_rows, gain).astype(BF16)
    key_rows = jnp.concatenate([k0_ref[...], k1_ref[...]], axis=0).astype(F32)
    key_rows = unit_rows(key_rows, gain).astype(BF16)
    scale = 1.0 / math.sqrt(64)
    totals = jnp.zeros((512, 128), F32)
    queries = jnp.dot(query_rows, wq_ref[...], preferred_element_type=F32)
    keys = jnp.dot(key_rows, wkv_ref[:, :512], preferred_element_type=F32)
    values = jnp.dot(key_rows, wkv_ref[:, 512:], preferred_element_type=F32)
    for g in range(4):
        at = 128 * g
        q = queries[:, at : at + 128]
        q = (head_norm(q, head_ref[0:1, :]) * scale).astype(BF16)
        k = keys[:, at : at + 128]
        k = head_norm(k, head_ref[1:2, :])
        v = values[:, at : at + 128]
        parts = []
        for side in range(2):
            own = even if side == 0 else jnp.logical_not(even)
            k_own = jnp.where(own, k, 0.0).astype(BF16)
            v_own = jnp.where(own, v, 1.0).astype(BF16)
            scores = lax.dot_general(q, k_own, (((1,), (1,)), ((), ())), preferred_element_type=F32)
            weights = jnp.exp(scores).astype(BF16)
            parts.append(jnp.dot(weights, v_own, preferred_element_type=F32))
        summed = jnp.where(even, parts[0], parts[1])
        total = jnp.where(even, parts[1], parts[0])
        high = total.astype(BF16).astype(F32)
        totals = totals + jnp.where(lane % 64 == 2 * g, high, jnp.where(lane % 64 == 2 * g + 1, total - high, 0.0))
        split_blocks(summed, keep_ref, send_ref, slice(at, at + 128))
    split_blocks(totals, keep_ref, send_ref, slice(512, 640))


def attention(q0, q1, ks, token_gain, head_gains, wq, wkv):
    head2 = jnp.concatenate([head_gains, head_gains], axis=1)
    return pl.pallas_call(
        attention_kernel,
        out_shape=(jax.ShapeDtypeStruct((256, 640), F32), jax.ShapeDtypeStruct((256, 640), BF16)),
        in_specs=[VMEM_SPEC] * 8,
        out_specs=(VMEM_SPEC, VMEM_SPEC),
        compiler_params=pltpu.CompilerParams(vmem_limit_bytes=16 << 20),
        name="attention",
    )(q0, q1, *ks, token_gain.reshape(1, 512), head2, wq, wkv)


def split_totals(x):
    lane = lax.broadcasted_iota(jnp.int32, (1, 128), 1)
    total = x + pltpu.roll(x, 127, 1)
    high = total.astype(BF16).astype(F32)
    return jnp.where(lane % 2 == 0, high, pltpu.roll(total - high, 1, 1))


def reduce_kernel(keep_ref, got_ref, out_ref, send_ref):
    total = keep_ref[...] + got_ref[...].astype(F32)
    if out_ref.shape[0] == send_ref.shape[0]:
        split_blocks(total[:, :512], out_ref, send_ref, slice(0, 512))
        even_out = [total[64 * i : 64 * i + 32, 512:] for i in range(total.shape[0] // 64)]
        odd_out = [total[64 * i + 32 : 64 * i + 64, 512:] for i in range(total.shape[0] // 64)]
        out_ref[:, 512:] = jnp.concatenate(even_out, axis=0)
        send_ref[:, 512:] = split_totals(jnp.concatenate(odd_out, axis=0)).astype(BF16)
    else:
        rows = out_ref.shape[0]
        out_ref[...] = total[:rows]
        send_ref[:, :512] = total[rows:, :512].astype(BF16)
        send_ref[:, 512:] = split_totals(total[rows:, 512:]).astype(BF16)


def reduce_step(keep, got, rows):
    count = keep.shape[0]
    return pl.pallas_call(
        reduce_kernel,
        out_shape=(jax.ShapeDtypeStruct((rows, 640), F32), jax.ShapeDtypeStruct((count - rows, 640), BF16)),
        in_specs=[VMEM_SPEC] * 2,
        out_specs=(VMEM_SPEC, VMEM_SPEC),
        compiler_params=pltpu.CompilerParams(vmem_limit_bytes=4 << 20),
        name="reduce_step",
    )(keep, got)


def final_kernel(keep_ref, g1_ref, g2_ref, g3_ref, tokens_ref, wo_ref, we_ref, s0_ref, s1_ref, out_ref, coarse_ref, lifted_ref, block_ref, sems):
    total = keep_ref[...] + g1_ref[...].astype(F32) + g2_ref[...].astype(F32) + g3_ref[...].astype(F32)
    r = lax.broadcasted_iota(jnp.int32, (128, 512), 0)
    head = lax.broadcasted_iota(jnp.int32, (128, 512), 1) // 64
    at = jnp.where(head % 2 == 1, 0, 64) + head // 2 * 2
    pick = jnp.where((r == at) | (r == at + 1), 1.0, 0.0).astype(BF16)
    high, low = high_low(total[:, 512:])
    spread = jnp.dot(high, pick, preferred_element_type=F32) + jnp.dot(low, pick, preferred_element_type=F32)
    attended = (total[:, :512] / spread).astype(BF16)
    coarse = tokens_ref[...].astype(F32) + jnp.dot(attended, wo_ref[...], preferred_element_type=F32)
    rounded = coarse.astype(BF16)
    lifted_ref[...] = jnp.dot(rounded, we_ref[...], preferred_element_type=F32)
    for a in range(8):
        coarse_ref[a] = coarse[4 * a : 4 * a + 4].astype(BF16)
    copies = []
    for a in range(8):
        for b in range(4):
            row = lifted_ref[4 * a + b : 4 * a + b + 1, :].reshape(1, 1, 128)
            cols = slice(16 * b, 16 * b + 16)
            half_ref, at = (s0_ref, 16 * a) if a < 4 else (s1_ref, 16 * a - 64)
            block_ref[a, :, cols] = (half_ref[at : at + 16, cols] + row).astype(BF16)
        copy = pltpu.make_async_copy(block_ref.at[a], out_ref.at[pl.ds(16 * a, 16)], sems.at[a])
        copy.start()
        copies.append(copy)
    for copy in copies:
        copy.wait()


def final(keep, got, tokens, wo, we, second):
    return pl.pallas_call(
        final_kernel,
        out_shape=(jax.ShapeDtypeStruct((128, 64, 128), BF16), jax.ShapeDtypeStruct((8, 4, 512), BF16)),
        in_specs=[VMEM_SPEC] * 9,
        out_specs=(ANY_SPEC, VMEM_SPEC),
        scratch_shapes=[pltpu.VMEM((32, 128), F32), pltpu.VMEM((8, 16, 64, 128), BF16), pltpu.SemaphoreType.DMA((8,))],
        compiler_params=pltpu.CompilerParams(vmem_limit_bytes=12 << 20),
        name="final",
    )(keep, *got, tokens, wo, we, *second)


AXES = ("lon", "lat")


def device_pairs(move):
    pairs = []
    for y in range(4):
        for zl in range(2):
            for c in range(2):
                for x in range(4):
                    for zh in range(4):
                        ty, tl, tc, tx, th = move(y, zl, c, x, zh)
                        source = ((y * 2 + zl) * 2 + c) * 16 + x * 4 + zh
                        target = ((ty * 2 + tl) * 2 + tc) * 16 + tx * 4 + th
                        pairs.append((source, target))
    return pairs


def move(value, y=0, low=0, core=0, x=0, high=0):
    return lax.ppermute(
        value, AXES,
        device_pairs(lambda a, b, c, d, e: (a ^ y, b ^ low, c ^ core, d ^ x, e ^ high)),
    )


def block(
    fine_state,
    coarse_state,
    norm_gains,
    kernels,
    token_gain,
    head_gains,
    query_weight,
    keyvalue_weight,
    output_weight,
    expand_weight,
):
    count = 16
    place = lax.axis_index("lon"), lax.axis_index("lat")
    even = [at % 2 == 0 for at in place]
    inner = [(i, i ^ 1) for i in range(count)]
    outer = [(i, (i + 1) % count if i % 2 else (i - 1) % count) for i in range(count)]
    top, bottom = fine_state[:2], fine_state[-2:]
    got_inner = lax.ppermute(jnp.where(even[0], bottom, top), "lon", inner)
    got_outer = lax.ppermute(jnp.where(even[0], top, bottom), "lon", outer)
    low = jnp.where(even[0], got_outer, got_inner)
    high = jnp.where(even[0], got_inner, got_outer)
    tokens = coarse_state.reshape(32, 512)
    near = jnp.concatenate([tokens, move(tokens, core=1)], axis=0)
    far = jnp.concatenate([tokens, move(tokens, high=1)], axis=0)
    first = jnp.concatenate([low[:, :2], fine_state[:, :2], high[:, :2]], axis=0)
    last = jnp.concatenate([low[:, -2:], fine_state[:, -2:], high[:, -2:]], axis=0)
    got_inner = lax.ppermute(jnp.where(even[1], last, first), "lat", inner)
    got_outer = lax.ppermute(jnp.where(even[1], first, last), "lat", outer[1:-1])
    left = jnp.where(even[1], got_outer, got_inner)
    right = jnp.where(even[1], got_inner, got_outer)
    near = jnp.concatenate([near, move(near, low=1)], axis=0)
    far = jnp.concatenate([far, move(far, high=2)], axis=0)
    rim = jnp.concatenate([right, jnp.zeros((132, 4, 128), BF16), left], axis=1)
    position = lax.broadcasted_iota(jnp.int32, (CIRCLE, 128), 0)
    column = place[1] * 64 + jnp.where(position < 68, position, position - CIRCLE)
    inside = jnp.where((column >= 0) & (column < 64 * count), 1.0, 0.0).astype(F32)
    hidden = []
    starts = (0, 25, 45, 65)

    def conv(k):
        hidden.append(
            first_conv(starts[k], starts[k + 1] - starts[k], fine_state, low, high, rim, kernels, norm_gains, inside)
        )

    conv(0)
    near = jnp.concatenate([near, move(near, y=1)], axis=0)
    far = jnp.concatenate([far, move(far, x=1)], axis=0)
    conv(1)
    across = move(near, y=2)
    key_tokens = [far, move(far, x=2)]
    conv(2)
    keep, out = attention(near, across, key_tokens, token_gain, head_gains, query_weight, keyvalue_weight)
    keep, out = reduce_step(keep, move(out, core=1), 128)
    got = move(out, low=1)
    second_a = second_conv(0, 32, starts[:2], hidden[:2], kernels, fine_state)
    keep, out = reduce_step(keep, got, 32)
    got = [move(out[32 * k - 32 : 32 * k], y=k) for k in (1, 2, 3)]
    second_b = second_conv(32, 32, starts[1:3], hidden[1:], kernels, fine_state)
    second = [half.reshape(64, 64, 128) for half in (second_a, second_b)]
    return final(keep, got, tokens, output_weight, expand_weight, second)


def solution(mesh):
    return jax.shard_map(
        block,
        mesh=mesh,
        in_specs=(
            P("lon", "lat", None),
            P("lon", "lat", None),
            P(),
            P(),
            P(),
            P(),
            P(),
            P(),
            P(),
            P(),
        ),
        out_specs=(P("lon", "lat", None), P("lon", "lat", None)),
        check_vma=False,
    )
```

```python
import functools
import math
import jax
import jax.numpy as jnp
from jax import lax
from jax.experimental import pallas as pl
from jax.experimental.pallas import tpu as pltpu

from jax.sharding import PartitionSpec as P


WIDE = 80
CIRCLE = 72
SHIFT_BLOCK = 5
F32 = jnp.float32
BF16 = jnp.bfloat16


def unit_rows(v, gain):
    return v * lax.rsqrt(jnp.mean(v * v, axis=-1, keepdims=True) + 1e-06) * gain


def pair_weights(taps_ref, pair_ref):
    zero = jnp.zeros((128, 128), BF16)
    for row in range(4):
        for b in range(3):
            at = (row * 3 + b) * 128
            pair_ref[at : at + 128, 0:128] = taps_ref[row, b] if row < 3 else zero
            pair_ref[at : at + 128, 128:256] = taps_ref[row - 1, b] if row > 0 else zero


def activate_rows(v, half_gain):
    half = v * (lax.rsqrt(jnp.mean(v * v, axis=-1, keepdims=True) + 1e-06) * half_gain)
    return half + half * jnp.tanh(half)


def store_shifted(hidden_ref, p, count, half, value, width):
    at = pl.ds(p, count)
    hidden_ref[0, at, half, :width] = pltpu.roll(value, 1, 1)[:, :width].astype(BF16)
    hidden_ref[1, at, half, :width] = value[:, :width].astype(BF16)
    hidden_ref[2, at, half, :width] = pltpu.roll(value, CIRCLE - 1, 1)[:, :width].astype(BF16)


def conv_pairs(hidden_ref, pair_ref, first, count, width):
    pieces = []
    for row in range(4):
        for b in range(3):
            at = first + row // 2
            piece = hidden_ref[b, at : at + count, row % 2]
            pieces.append(piece.reshape(count * width, 128))
    return jnp.dot(
        jnp.concatenate(pieces, axis=1), pair_ref[...], preferred_element_type=F32
    )


def first_conv_kernel(begin, count, fine_ref, low_ref, high_ref, rim_ref, taps_ref, gains_ref, inside_ref, out_ref, hidden_ref, pair_ref):
    lower, upper = max(begin, 1), min(begin + count + 1, 65)
    block = next(n for n in (5, 7) if (upper - lower) % n == 0)
    taps, gains = taps_ref.at[0], gains_ref
    half_gain = 0.5 * gains[0:1, :].reshape(1, 1, 128)

    def activate(main, rim, p, count):
        row = jnp.concatenate([main.astype(F32), rim.astype(F32)], axis=1)
        row = activate_rows(row, half_gain).reshape(count, 2, CIRCLE, 128)
        for half in range(2):
            store_shifted(hidden_ref, p - begin, count, half, row[:, half], CIRCLE)

    if begin == 0:
        activate(low_ref[...], rim_ref[0:2], 0, 1)
    if begin + count == 65:
        activate(high_ref[...], rim_ref[130:132], 65, 1)
    for p in range(lower, upper, block):
        activate(fine_ref[2 * p - 2 : 2 * p - 2 + 2 * block], rim_ref[2 * p : 2 * p + 2 * block], p, block)
    pair_weights(taps, pair_ref)
    second_half_gain = 0.5 * gains[1:2, :].reshape(1, 1, 128)
    inside = inside_ref[...].reshape(1, CIRCLE, 128)
    for first in range(0, count, 5):
        both = conv_pairs(hidden_ref, pair_ref, first, 5, WIDE)
        for half in range(2):
            value = both[:, 128 * half : 128 * half + 128].reshape(5, WIDE, 128)[:, :CIRCLE]
            value = activate_rows(value, second_half_gain) * inside
            out_ref[first : first + 5, half] = value.astype(BF16)


VMEM_SPEC = pl.BlockSpec(memory_space=pltpu.VMEM)
ANY_SPEC = pl.BlockSpec(memory_space=pl.ANY)


def first_conv(begin, count, fine, low, high, rim, kernels, gains, inside):
    return pl.pallas_call(
        functools.partial(first_conv_kernel, begin, count),
        out_shape=jax.ShapeDtypeStruct((count, 2, CIRCLE, 128), BF16),
        in_specs=[VMEM_SPEC] * 7,
        out_specs=VMEM_SPEC,
        scratch_shapes=[
            pltpu.VMEM((3, count + 1, 2, WIDE, 128), BF16),
            pltpu.VMEM((1536, 256), BF16),
        ],
        compiler_params=pltpu.CompilerParams(vmem_limit_bytes=12 << 20),
        name="first_conv",
    )(fine, low, high, rim, kernels, gains, inside)


def second_conv_kernel(begin, pairs, starts, *refs):
    hidden_refs, (taps_ref, fine_ref, out_ref, hidden_ref, pair_ref) = refs[:-5], refs[-5:]
    pair_weights(taps_ref.at[1], pair_ref)
    for ref, start in zip(hidden_refs, starts):
        lower, upper = max(start, begin), min(start + ref.shape[0], begin + pairs + 1)
        for p in range(lower, upper, SHIFT_BLOCK):
            count = min(SHIFT_BLOCK, upper - p)
            for half in range(2):
                value = ref[p - start : p - start + count, half].astype(F32)
                store_shifted(hidden_ref, p - begin, count, half, value, 64)

    for first in range(0, pairs, 8):
        both = conv_pairs(hidden_ref, pair_ref, first, 8, 64)
        for half in range(2):
            value = both[:, 128 * half : 128 * half + 128].reshape(8, 64, 128)
            out_ref[first : first + 8, half] = value + fine_ref[begin + first : begin + first + 8, half].astype(F32)


def second_conv(begin, pairs, starts, hidden, kernels, fine):
    return pl.pallas_call(
        functools.partial(second_conv_kernel, begin, pairs, starts),
        out_shape=jax.ShapeDtypeStruct((pairs, 2, 64, 128), F32),
        in_specs=[VMEM_SPEC] * (len(hidden) + 2),
        out_specs=VMEM_SPEC,
        scratch_shapes=[pltpu.VMEM((3, pairs + 1, 2, 64, 128), BF16), pltpu.VMEM((1536, 256), BF16)],
        compiler_params=pltpu.CompilerParams(vmem_limit_bytes=12 << 20),
        name="second_conv",
    )(*hidden, kernels, fine.reshape(64, 2, 64, 128))


def high_low(v):
    high = v.astype(BF16)
    return high, (v - high.astype(F32)).astype(BF16)


def split_blocks(value, keep_ref, send_ref, columns):
    for i in range(value.shape[0] // 64):
        keep_ref[32 * i : 32 * i + 32, columns] = value[64 * i : 64 * i + 32]
        send_ref[32 * i : 32 * i + 32, columns] = value[64 * i + 32 : 64 * i + 64].astype(BF16)


def attention_kernel(q0_ref, q1_ref, k0_ref, k1_ref, gain_ref, head_ref, wq_ref, wkv_ref, keep_ref, send_ref):
    gain = gain_ref[...]
    lane = lax.broadcasted_iota(jnp.int32, (1, 128), 1)
    even = lane < 64

    def head_norm(v, head_gain):
        square = v * v
        sums = [jnp.sum(jnp.where(own, square, 0.0), axis=-1, keepdims=True) for own in (even, jnp.logical_not(even))]
        mean = jnp.where(even, sums[0], sums[1]) * (1.0 / 64)
        return v * lax.rsqrt(mean + 1e-06) * head_gain

    query_rows = jnp.concatenate([q0_ref[...], q1_ref[...]], axis=0).astype(F32)
    query_rows = unit_rows(query_rows, gain).astype(BF16)
    key_rows = jnp.concatenate([k0_ref[...], k1_ref[...]], axis=0).astype(F32)
    key_rows = unit_rows(key_rows, gain).astype(BF16)
    scale = 1.0 / math.sqrt(64)
    totals = jnp.zeros((512, 128), F32)
    queries = jnp.dot(query_rows, wq_ref[...], preferred_element_type=F32)
    keys = jnp.dot(key_rows, wkv_ref[:, :512], preferred_element_type=F32)
    values = jnp.dot(key_rows, wkv_ref[:, 512:], preferred_element_type=F32)
    for g in range(4):
        at = 128 * g
        q = queries[:, at : at + 128]
        q = (head_norm(q, head_ref[0:1, :]) * scale).astype(BF16)
        k = keys[:, at : at + 128]
        k = head_norm(k, head_ref[1:2, :])
        v = values[:, at : at + 128]
        parts = []
        for side in range(2):
            own = even if side == 0 else jnp.logical_not(even)
            k_own = jnp.where(own, k, 0.0).astype(BF16)
            v_own = jnp.where(own, v, 1.0).astype(BF16)
            scores = lax.dot_general(q, k_own, (((1,), (1,)), ((), ())), preferred_element_type=F32)
            weights = jnp.exp(scores).astype(BF16)
            parts.append(jnp.dot(weights, v_own, preferred_element_type=F32))
        summed = jnp.where(even, parts[0], parts[1])
        total = jnp.where(even, parts[1], parts[0])
        high = total.astype(BF16).astype(F32)
        totals = totals + jnp.where(lane % 64 == 2 * g, high, jnp.where(lane % 64 == 2 * g + 1, total - high, 0.0))
        split_blocks(summed, keep_ref, send_ref, slice(at, at + 128))
    split_blocks(totals, keep_ref, send_ref, slice(512, 640))


def attention(q0, q1, ks, token_gain, head_gains, wq, wkv):
    head2 = jnp.concatenate([head_gains, head_gains], axis=1)
    return pl.pallas_call(
        attention_kernel,
        out_shape=(jax.ShapeDtypeStruct((256, 640), F32), jax.ShapeDtypeStruct((256, 640), BF16)),
        in_specs=[VMEM_SPEC] * 8,
        out_specs=(VMEM_SPEC, VMEM_SPEC),
        compiler_params=pltpu.CompilerParams(vmem_limit_bytes=16 << 20),
        name="attention",
    )(q0, q1, *ks, token_gain.reshape(1, 512), head2, wq, wkv)


def split_totals(x):
    lane = lax.broadcasted_iota(jnp.int32, (1, 128), 1)
    total = x + pltpu.roll(x, 127, 1)
    high = total.astype(BF16).astype(F32)
    return jnp.where(lane % 2 == 0, high, pltpu.roll(total - high, 1, 1))


def reduce_kernel(keep_ref, got_ref, out_ref, send_ref):
    total = keep_ref[...] + got_ref[...].astype(F32)
    if out_ref.shape[0] == send_ref.shape[0]:
        split_blocks(total[:, :512], out_ref, send_ref, slice(0, 512))
        even_out = [total[64 * i : 64 * i + 32, 512:] for i in range(total.shape[0] // 64)]
        odd_out = [total[64 * i + 32 : 64 * i + 64, 512:] for i in range(total.shape[0] // 64)]
        out_ref[:, 512:] = jnp.concatenate(even_out, axis=0)
        send_ref[:, 512:] = split_totals(jnp.concatenate(odd_out, axis=0)).astype(BF16)
    else:
        rows = out_ref.shape[0]
        out_ref[...] = total[:rows]
        send_ref[:, :512] = total[rows:, :512].astype(BF16)
        send_ref[:, 512:] = split_totals(total[rows:, 512:]).astype(BF16)


def reduce_step(keep, got, rows):
    count = keep.shape[0]
    return pl.pallas_call(
        reduce_kernel,
        out_shape=(jax.ShapeDtypeStruct((rows, 640), F32), jax.ShapeDtypeStruct((count - rows, 640), BF16)),
        in_specs=[VMEM_SPEC] * 2,
        out_specs=(VMEM_SPEC, VMEM_SPEC),
        compiler_params=pltpu.CompilerParams(vmem_limit_bytes=4 << 20),
        name="reduce_step",
    )(keep, got)


def final_kernel(keep_ref, g1_ref, g2_ref, g3_ref, tokens_ref, wo_ref, we_ref, s0_ref, s1_ref, out_ref, coarse_ref, lifted_ref, block_ref, sems):
    total = keep_ref[...] + g1_ref[...].astype(F32) + g2_ref[...].astype(F32) + g3_ref[...].astype(F32)
    r = lax.broadcasted_iota(jnp.int32, (128, 512), 0)
    head = lax.broadcasted_iota(jnp.int32, (128, 512), 1) // 64
    at = jnp.where(head % 2 == 1, 0, 64) + head // 2 * 2
    pick = jnp.where((r == at) | (r == at + 1), 1.0, 0.0).astype(BF16)
    high, low = high_low(total[:, 512:])
    spread = jnp.dot(high, pick, preferred_element_type=F32) + jnp.dot(low, pick, preferred_element_type=F32)
    attended = (total[:, :512] / spread).astype(BF16)
    coarse = tokens_ref[...].astype(F32) + jnp.dot(attended, wo_ref[...], preferred_element_type=F32)
    rounded = coarse.astype(BF16)
    lifted_ref[...] = jnp.dot(rounded, we_ref[...], preferred_element_type=F32)
    for a in range(8):
        coarse_ref[a] = coarse[4 * a : 4 * a + 4].astype(BF16)
    copies = []
    for a in range(8):
        for b in range(4):
            row = lifted_ref[4 * a + b : 4 * a + b + 1, :].reshape(1, 1, 128)
            cols = slice(16 * b, 16 * b + 16)
            half_ref, at = (s0_ref, 16 * a) if a < 4 else (s1_ref, 16 * a - 64)
            block_ref[a, :, cols] = (half_ref[at : at + 16, cols] + row).astype(BF16)
        copy = pltpu.make_async_copy(block_ref.at[a], out_ref.at[pl.ds(16 * a, 16)], sems.at[a])
        copy.start()
        copies.append(copy)
    for copy in copies:
        copy.wait()


def final(keep, got, tokens, wo, we, second):
    return pl.pallas_call(
        final_kernel,
        out_shape=(jax.ShapeDtypeStruct((128, 64, 128), BF16), jax.ShapeDtypeStruct((8, 4, 512), BF16)),
        in_specs=[VMEM_SPEC] * 9,
        out_specs=(ANY_SPEC, VMEM_SPEC),
        scratch_shapes=[pltpu.VMEM((32, 128), F32), pltpu.VMEM((8, 16, 64, 128), BF16), pltpu.SemaphoreType.DMA((8,))],
        compiler_params=pltpu.CompilerParams(vmem_limit_bytes=12 << 20),
        name="final",
    )(keep, *got, tokens, wo, we, *second)


AXES = ("lon", "lat")


def device_pairs(move):
    pairs = []
    for y in range(4):
        for zl in range(2):
            for c in range(2):
                for x in range(4):
                    for zh in range(4):
                        ty, tl, tc, tx, th = move(y, zl, c, x, zh)
                        source = ((y * 2 + zl) * 2 + c) * 16 + x * 4 + zh
                        target = ((ty * 2 + tl) * 2 + tc) * 16 + tx * 4 + th
                        pairs.append((source, target))
    return pairs


def move(value, y=0, low=0, core=0, x=0, high=0):
    return lax.ppermute(
        value, AXES,
        device_pairs(lambda a, b, c, d, e: (a ^ y, b ^ low, c ^ core, d ^ x, e ^ high)),
    )


def block(
    fine_state,
    coarse_state,
    norm_gains,
    kernels,
    token_gain,
    head_gains,
    query_weight,
    keyvalue_weight,
    output_weight,
    expand_weight,
):
    count = 16
    place = lax.axis_index("lon"), lax.axis_index("lat")
    even = [at % 2 == 0 for at in place]
    inner = [(i, i ^ 1) for i in range(count)]
    outer = [(i, (i + 1) % count if i % 2 else (i - 1) % count) for i in range(count)]
    top, bottom = fine_state[:2], fine_state[-2:]
    got_inner = lax.ppermute(jnp.where(even[0], bottom, top), "lon", inner)
    got_outer = lax.ppermute(jnp.where(even[0], top, bottom), "lon", outer)
    low = jnp.where(even[0], got_outer, got_inner)
    high = jnp.where(even[0], got_inner, got_outer)
    tokens = coarse_state.reshape(32, 512)
    near = jnp.concatenate([tokens, move(tokens, core=1)], axis=0)
    far = jnp.concatenate([tokens, move(tokens, high=1)], axis=0)
    first = jnp.concatenate([low[:, :2], fine_state[:, :2], high[:, :2]], axis=0)
    last = jnp.concatenate([low[:, -2:], fine_state[:, -2:], high[:, -2:]], axis=0)
    got_inner = lax.ppermute(jnp.where(even[1], last, first), "lat", inner)
    got_outer = lax.ppermute(jnp.where(even[1], first, last), "lat", outer[1:-1])
    left = jnp.where(even[1], got_outer, got_inner)
    right = jnp.where(even[1], got_inner, got_outer)
    near = jnp.concatenate([near, move(near, low=1)], axis=0)
    far = jnp.concatenate([far, move(far, high=3)], axis=0)
    rim = jnp.concatenate([right, jnp.zeros((132, 4, 128), BF16), left], axis=1)
    position = lax.broadcasted_iota(jnp.int32, (CIRCLE, 128), 0)
    column = place[1] * 64 + jnp.where(position < 68, position, position - CIRCLE)
    inside = jnp.where((column >= 0) & (column < 64 * count), 1.0, 0.0).astype(F32)
    hidden = []
    starts = (0, 15, 35, 65)

    def conv(k):
        hidden.append(
            first_conv(starts[k], starts[k + 1] - starts[k], fine_state, low, high, rim, kernels, norm_gains, inside)
        )

    conv(0)
    near = jnp.concatenate([near, move(near, y=1)], axis=0)
    far = jnp.concatenate([far, move(far, x=1)], axis=0)
    conv(1)
    across = move(near, y=3)
    key_tokens = [far, move(far, x=3)]
    conv(2)
    keep, out = attention(near, across, key_tokens, token_gain, head_gains, query_weight, keyvalue_weight)
    keep, out = reduce_step(keep, move(out, core=1), 128)
    got = move(out, low=1)
    second_a = second_conv(0, 32, starts[:2], hidden[:2], kernels, fine_state)
    keep, out = reduce_step(keep, got, 32)
    got = [move(out[32 * i : 32 * i + 32], y=k) for i, k in enumerate((1, 3, 2))]
    second_b = second_conv(32, 32, starts[1:3], hidden[1:], kernels, fine_state)
    second = [half.reshape(64, 64, 128) for half in (second_a, second_b)]
    return final(keep, got, tokens, output_weight, expand_weight, second)


def solution(mesh):
    return jax.shard_map(
        block,
        mesh=mesh,
        in_specs=(
            P("lon", "lat", None),
            P("lon", "lat", None),
            P(),
            P(),
            P(),
            P(),
            P(),
            P(),
            P(),
            P(),
        ),
        out_specs=(P("lon", "lat", None), P("lon", "lat", None)),
        check_vma=False,
    )
```
